128 devices in a mesh: tgt: 4 (over y_hi, core), feat: 16 (over z, x), dp: 2 (over y_lo).
Axes of the slice: x: 4, y: 4 (y_hi: 2, y_lo: 2; y = y_hi * 2 + y_lo), z: 4, core: 2. Of those that a mesh axis runs over, the one named last changes fastest.
Arguments:
- source: bfloat16 [1536, 4096], P('dp', 'tgt'), may hold values from -6 to 6
- targets: bfloat16 [4, 1536, 4096], P('tgt', 'dp'), may hold values from -6 to 6
- encoder_weight: bfloat16 [4096, 16384], P('tgt', 'feat'), may hold values from -0.09375 to 0.09375
- encoder_bias: bfloat16 [16384], P('feat'), may hold values from -1 to 0.5
- decoder_weight: bfloat16 [4, 16384, 4096], P('tgt', 'feat'), may hold values from -1.14819832 to 1.14819832, as said below
Outputs:
- rebuilt: bfloat16 [4, 1536, 4096], P('tgt', 'dp', 'feat')
- encoder_grad: float32 [4096, 16384], P(('tgt', 'dp'), 'feat')
- bias_grad: float32 [16384], P(('feat', 'dp'))
- decoder_grad: float32 [4, 16384, 4096], P('tgt', 'feat', 'dp')
The draws below stay inside these ranges and needn't reach their ends.
Inputs may be any that keep to these rules, and one draw needn't show every extreme that they name: The entries of decoder_weight have scales that differ by feature, by column and by target layer.
All inputs are finite; a program needn't handle non-finite values.
Results may differ from the reference program's by a relative error of at most 0.015.
Values may be sent and summed in bfloat16 or wider, within the bound.
No kernel may reach another device: no remote copies, remote signals or barrier semaphores. Data moves between devices by JAX's collectives and lax.ppermute only.
A program may use at most 128 MiB of HBM per device.

```python
import math
import jax
import jax.numpy as jnp
from jax import lax

D = 4096
F = 16384
TGT_LAYERS = 4
TOKENS = 1536
N_DP = 2


def draw_decoder_weight(key, part):
    first, second, third = jax.random.split(jax.random.fold_in(key, 71), 3)
    base = jnp.clip(jax.random.normal(first, (TGT_LAYERS, F, D), jnp.float32), -6.0, 6.0)
    rows = jnp.exp(jax.random.uniform(second, (1, F, 1), jnp.float32, -1.15, 1.15))
    columns = jnp.exp(jax.random.uniform(third, (1, 1, D), jnp.float32, -1.15, 1.15)) / 1.47
    steps = jnp.arange(TGT_LAYERS).astype(jnp.float32) / (TGT_LAYERS - 1)
    layer_scale = jnp.power(3.0, steps) / 1.7
    scale = layer_scale[:, None, None] * rows * columns / jnp.sqrt(1.5 * F)
    return (base * scale).astype(jnp.bfloat16)


def steps_of(stream_key, shape, pieces, smallest, largest):
    factor_of, own = 1.0, jax.random.fold_in(stream_key, 6)
    for position, shards_of in pieces:
        draws = jnp.exp(jax.random.uniform(jax.random.fold_in(own, position), (shards_of,), jnp.float32, smallest / len(pieces), largest / len(pieces)))
        factor_of = factor_of * jnp.repeat(draws, shape[position] // shards_of).reshape([-1 if axis == position else 1 for axis in range(len(shape))])
    return factor_of


def gaussian(stream_key, dims, width, most, shards=(), held_as=jnp.bfloat16):
    result = width * jax.random.normal(stream_key, dims, jnp.float32)
    if shards:
        result = result * steps_of(stream_key, dims, shards, -0.22, 0.18)
    return jnp.clip(result, -most, most).astype(held_as)


def setup_inputs(seed: int = 0) -> dict:
    key_list = jax.random.split(jax.random.key(seed), 6)
    return {
        "source": gaussian(key_list[0], (TOKENS, D), 1.0, 6.0, ((0, 2), (1, 4))),
        "targets": gaussian(key_list[1], (TGT_LAYERS, TOKENS, D), 1.0, 6.0, ((0, 4), (1, 2))),
        "encoder_weight": gaussian(key_list[2], (D, F), D ** -0.5, 0.09375, ((0, 4), (1, 16))),
        "encoder_bias": jnp.clip(-1.0 + 1.5 * jax.random.uniform(key_list[3], (F,), jnp.float32) ** steps_of(key_list[3], (F,), ((0, 16),), -0.2, 0.2), -1.0, 0.5).astype(jnp.bfloat16),
        "decoder_weight": draw_decoder_weight(jax.random.fold_in(key_list[5], 71), 0),
    }


sparsity_weight = 2.0

def transposed_product(left, right):
    return lax.dot_general(left, right, (((0,), (0,)), ((), ())), preferred_element_type=jnp.float32)

def reference(source, targets, encoder_weight, encoder_bias, decoder_weight):
    total = source.shape[0]
    scale_root = 1.0 / math.sqrt(total)
    preact = jnp.dot(source, encoder_weight, preferred_element_type=jnp.float32) + encoder_bias.astype(jnp.float32)
    active = jnp.maximum(preact, 0.0)
    feature_acts = (active * active).astype(jnp.bfloat16)
    norm_squares = jnp.zeros((decoder_weight.shape[1],), jnp.float32)
    for layer in range(TGT_LAYERS):
        norm_squares = norm_squares + lax.optimization_barrier(jnp.sum(jnp.square(decoder_weight[layer].astype(jnp.float32)), axis=1))
    norms = jnp.sqrt(norm_squares + 1e-06)
    rebuilt_list = []
    grad_list = []
    feature_grad = jnp.zeros((total, decoder_weight.shape[1]), jnp.float32)
    for layer in range(TGT_LAYERS):
        full = jnp.dot(feature_acts, decoder_weight[layer], preferred_element_type=jnp.float32)
        rebuilt_list.append(full.astype(jnp.bfloat16))
        rebuilt_grad = ((full - targets[layer].astype(jnp.float32)) * scale_root).astype(jnp.bfloat16)
        grad_list.append(rebuilt_grad)
        feature_grad = feature_grad + lax.dot_general(rebuilt_grad, decoder_weight[layer], (((1,), (1,)), ((), ())), preferred_element_type=jnp.float32)
    feature_grad = feature_grad + sparsity_weight * scale_root * norms
    pre_grad = (feature_grad * 2.0 * active).astype(jnp.bfloat16)
    encoder_grad = transposed_product(source, pre_grad)
    bias_grad = lax.optimization_barrier(jnp.sum(pre_grad.astype(jnp.float32), axis=0))
    half = total // N_DP
    decoder_grads = []
    for layer in range(TGT_LAYERS):
        summed = jnp.zeros(decoder_weight.shape[1:], jnp.float32)
        for portion in range(N_DP):
            acts_part = feature_acts[portion * half:(portion + 1) * half]
            grad_part = grad_list[layer][portion * half:(portion + 1) * half]
            usage = lax.optimization_barrier(jnp.sum(acts_part.astype(jnp.float32), axis=0))
            shrink = sparsity_weight * scale_root * usage / norms
            term = transposed_product(acts_part, grad_part) + shrink[:, None] * decoder_weight[layer].astype(jnp.float32)
            rounded = lax.optimization_barrier(term.astype(jnp.bfloat16))
            summed = summed + rounded.astype(jnp.float32)
        decoder_grads.append(summed)
    return (jnp.stack(rebuilt_list), encoder_grad, bias_grad, jnp.stack(decoder_grads))
```

```python
import math

import jax
import jax.numpy as jnp
from jax import lax
from jax.sharding import Mesh, PartitionSpec as P

sparsity_weight = 2.0

bf16 = jnp.bfloat16
f32 = jnp.float32
Y = ("yh", "yl")


def shift(value, axis, size, step):
    return lax.ppermute(value, axis, [(i, (i + step) % size) for i in range(size)])


def mm(left, right):
    return jnp.dot(left, right, preferred_element_type=f32)


def pick(value, index, axis=0):
    return lax.dynamic_index_in_dim(value, index, axis, keepdims=False)


def gather_y(block):
    ahead = shift(block, Y, 4, -1)
    behind = shift(block, Y, 4, 1)
    opposite = shift(block, Y, 4, 2)
    return jnp.concatenate([block, ahead, opposite, behind], axis=0)


def big_scatter(axis, part):
    up = shift(part(2, 0).astype(bf16), axis, 4, 1)
    down = shift(part(2, 1).astype(bf16), axis, 4, -1)
    raw_up = shift(part(1, 1).astype(bf16), axis, 4, 1)
    raw_down = shift(part(3, 0).astype(bf16), axis, 4, -1)
    mine_up, mine_down = part(1, 0).astype(bf16), part(3, 1).astype(bf16)
    mine_up, mine_down = lax.optimization_barrier((mine_up, mine_down))
    sum_up = shift((mine_up.astype(f32) + up.astype(f32)).astype(bf16), axis, 4, 1)
    sum_down = shift((mine_down.astype(f32) + down.astype(f32)).astype(bf16), axis, 4, -1)
    own = lax.optimization_barrier((part(0, 0), part(0, 1)))
    return (
        own[0] + sum_up.astype(f32) + raw_down.astype(f32),
        own[1] + raw_up.astype(f32) + sum_down.astype(f32),
    )


def small_scatter(axis, chunk):
    one = shift(chunk(1).astype(bf16), axis, 4, 1)
    three = shift(chunk(3).astype(bf16), axis, 4, -1)
    two = shift(chunk(2).astype(bf16), axis, 4, 2)
    return chunk(0) + one.astype(f32) + two.astype(f32) + three.astype(f32)


def small_gather(axis, block):
    one = shift(block, axis, 4, -1)
    three = shift(block, axis, 4, 1)
    two = shift(block, axis, 4, 2)
    return ((0, block), (1, one), (2, two), (3, three))


def big_gather(axis, first, second):
    behind_first = shift(first, axis, 4, 1)
    ahead_second = shift(second, axis, 4, -1)
    behind_second = shift(second, axis, 4, 1)
    ahead_first = shift(first, axis, 4, -1)
    far_first = shift(behind_first, axis, 4, 1)
    far_second = shift(ahead_second, axis, 4, -1)
    return (
        (0, 0, first),
        (0, 1, second),
        (1, 0, ahead_first),
        (1, 1, ahead_second),
        (3, 0, behind_first),
        (3, 1, behind_second),
        (2, 0, far_first),
        (2, 1, far_second),
    )


def body(source, targets, encoder_weight, encoder_bias, decoder_weight):
    yh, core, z, x, yl = (lax.axis_index(a) for a in ("yh", "core", "z", "x", "yl"))
    half_tokens, width = source.shape
    block = half_tokens // 4
    features, columns = decoder_weight.shape[1:]
    half_columns = columns // 2
    part_columns = half_columns // 4
    scale_root = 1.0 / math.sqrt(half_tokens * 2)
    decoder = decoder_weight[0]
    target_rows = targets[0]
    column_start = yl * half_columns

    def columns_of(k):
        return lax.dynamic_slice(
            decoder, (0, column_start + part_columns * ((x + k) % 4)), (features, part_columns)
        )

    source_parts = source.reshape(2, 2, block, width)
    sent = mm(pick(source_parts, 1 - core, 1).reshape(2 * block, width), encoder_weight).astype(bf16)
    kept = mm(pick(source_parts, core, 1).reshape(2 * block, width), encoder_weight)
    sent = shift(sent, "core", 2, 1)
    both = (kept + sent.astype(f32)).reshape(2, block, features)
    other = shift(pick(both, 1 - yh).astype(bf16), "yh", 2, 1)
    preact = pick(both, yh) + other.astype(f32) + encoder_bias.astype(f32)
    active = jnp.maximum(preact, 0.0)
    acts_own = gather_y((active * active).astype(bf16))
    acts_other = shift(acts_own, "core", 2, 1)

    target_other = lax.dynamic_slice(
        target_rows,
        ((yh ^ (1 - yl) ^ (z // 2)) * 2 * block, (1 - yl) * half_columns + part_columns * x),
        (2 * block, part_columns),
    )
    pairs = [(q * 2 + i, q * 2 + 1 - i) for q in (1, 3) for i in range(2)]
    target_other = lax.ppermute(target_other, ("z", "yl"), pairs)
    target_own = lax.dynamic_slice(
        target_rows,
        ((yh ^ (z // 2)) * 2 * block, column_start + part_columns * x),
        (2 * block, part_columns),
    )
    target_block = jnp.where(z % 2 == 1, target_other, target_own).reshape(2, block, part_columns)
    half_width = width // 2
    source_mine = lax.dynamic_slice_in_dim(source, yl * half_width, half_width, 1)
    source_theirs = shift(
        lax.dynamic_slice_in_dim(source, (1 - yl) * half_width, half_width, 1), "yl", 2, 1
    )
    source_mine = source_mine.reshape(2, 2, block, half_width)
    source_theirs = source_theirs.reshape(2, 2, block, half_width)
    slots = (
        pick(source_mine, yh),
        pick(source_theirs, yh ^ yl),
        pick(source_mine, 1 - yh),
        pick(source_theirs, 1 - (yh ^ yl)),
    )
    source_own = jnp.concatenate([pick(s, core) for s in slots], axis=0)
    source_other = jnp.concatenate([pick(s, 1 - core) for s in slots], axis=0)

    squares = jnp.sum(jnp.square(decoder.astype(f32)), axis=1)
    squares = squares + shift(squares, "core", 2, 1)
    squares = squares + shift(squares, "yh", 2, 1)
    norms = jnp.sqrt(squares + 1e-06)

    def own_part(k, h):
        rows = acts_own[h * 2 * block : (h + 1) * 2 * block]
        return mm(rows, columns_of(k))

    def other_part(k, h):
        rows = lax.dynamic_slice_in_dim(acts_other, ((z + k) % 4) * block, block, 0)
        cols = lax.dynamic_slice_in_dim(
            decoder, column_start + h * (half_columns // 2), half_columns // 2, 1
        )
        return mm(rows, cols)

    own_sum = jnp.concatenate(big_scatter("x", own_part), axis=0).reshape(4, block, part_columns)
    other_sum = jnp.concatenate(big_scatter("z", other_part), axis=1)
    full_own = small_scatter("z", lambda k: pick(own_sum, (z + k) % 4))
    full_other = small_scatter(
        "x",
        lambda k: lax.dynamic_slice_in_dim(
            other_sum, ((x + k) % 4) * part_columns, part_columns, 1
        ),
    )
    grad_own = ((full_own - pick(target_block, core).astype(f32)) * scale_root).astype(bf16)
    grad_other = ((full_other - pick(target_block, 1 - core).astype(f32)) * scale_root).astype(bf16)

    own_rows = jnp.zeros((4 * block, part_columns), bf16)
    for k, piece in small_gather("z", grad_own):
        own_rows = lax.dynamic_update_slice(own_rows, piece, (((z + k) % 4) * block, 0))
    other_cols = jnp.zeros((block, half_columns), bf16)
    for k, piece in small_gather("x", grad_other):
        other_cols = lax.dynamic_update_slice(other_cols, piece, (0, ((x + k) % 4) * part_columns))
    grad = jnp.zeros((8 * block, half_columns), bf16)
    for k, h, piece in big_gather("x", own_rows[: 2 * block], own_rows[2 * block :]):
        grad = lax.dynamic_update_slice(
            grad, piece, (h * 2 * block, ((x + k) % 4) * part_columns)
        )
    for k, h, piece in big_gather("z", other_cols[: block // 2], other_cols[block // 2 :]):
        grad = lax.dynamic_update_slice(
            grad, piece, (4 * block + ((z + k) % 4) * block + h * (block // 2), 0)
        )

    decoder_half = lax.dynamic_slice_in_dim(decoder, column_start, half_columns, 1)
    contract = (((1,), (1,)), ((), ()))

    def feature_part(rows):
        return lax.dot_general(rows, decoder_half, contract, preferred_element_type=f32)

    theirs = shift(feature_part(grad[4 * block :]).astype(bf16), "core", 2, 1)
    ours = feature_part(grad[: 4 * block]) + theirs.astype(f32)
    feature_grad = small_scatter(Y, lambda k: ours[k * block : (k + 1) * block])
    penalty = sparsity_weight * scale_root * norms
    pre_grad = ((feature_grad + penalty) * 2.0 * active).astype(bf16)
    pre_own = gather_y(pre_grad)
    pre_other = shift(pre_own, "core", 2, 1)

    def transposed(left, right):
        return lax.dot_general(
            left, right, (((0,), (0,)), ((), ())), preferred_element_type=f32
        )

    encoder_grad = transposed(source_own, pre_own) + transposed(source_other, pre_other)
    bias_sum = jnp.sum(pre_own.astype(f32), axis=0) + jnp.sum(pre_other.astype(f32), axis=0)
    bias_grad = lax.dynamic_slice_in_dim(bias_sum, yl * (features // 2), features // 2, 0)

    acts = jnp.concatenate([acts_own, acts_other], axis=0)
    usage = jnp.sum(acts.astype(f32), axis=0)
    shrink = sparsity_weight * scale_root * usage / norms
    decoder_grad = transposed(acts, grad) + shrink[:, None] * decoder_half.astype(f32)

    rebuilt_block = jnp.concatenate([full_own, full_other], axis=0).astype(bf16)
    rebuilt_block = rebuilt_block.reshape(2 * block, 2, part_columns // 2)
    rebuilt = jnp.zeros((half_tokens, part_columns // 2), bf16)
    for k in range(2):
        perm = []
        for zi in range(4):
            for xi in range(4):
                for yi in range(2):
                    s = (zi // 2) ^ k
                    to = ((2 * yi + xi // 2) * 4 + 2 * (xi % 2) + s) * 2 + (yi ^ (zi % 2))
                    perm.append(((zi * 4 + xi) * 2 + yi, to))
        piece = lax.ppermute(pick(rebuilt_block, (z // 2) ^ k, 1), ("z", "x", "yl"), perm)
        sender = z // 2
        rank = (x % 2) ^ k
        quarter = yh ^ rank ^ ((sender ^ yl) & sender)
        rebuilt = lax.dynamic_update_slice(
            rebuilt, piece[:block], (quarter * 2 * block + core * block, 0)
        )
        rebuilt = lax.dynamic_update_slice(
            rebuilt, piece[block:], (quarter * 2 * block + (1 - core) * block, 0)
        )
    return rebuilt[None], encoder_grad, bias_grad, decoder_grad[None]


def solution(mesh):
    fine = Mesh(mesh.devices.reshape(2, 2, 4, 4, 2), ("yh", "core", "z", "x", "yl"))
    tgt, feat = ("yh", "core"), ("z", "x")
    return jax.shard_map(
        body,
        mesh=fine,
        in_specs=(P("yl", tgt), P(tgt, "yl", None), P(tgt, feat), P(feat), P(tgt, feat, None)),
        out_specs=(
            P(tgt, "yl", feat),
            P(("yh", "core", "yl"), feat),
            P(("z", "x", "yl")),
            P(tgt, feat, "yl"),
        ),
        check_vma=False,
    )
```

```python
import math

import jax
import jax.numpy as jnp
from jax import lax
from jax.sharding import Mesh, PartitionSpec as P


sparsity_weight = 2.0

bf16 = jnp.bfloat16
f32 = jnp.float32
Y = ("yh", "yl")


def shift(value, axis, size, step):
    return lax.ppermute(value, axis, [(i, (i + step) % size) for i in range(size)])


def mm(left, right):
    return jnp.dot(left, right, preferred_element_type=f32)


def pick(value, index, axis=0):
    return lax.dynamic_index_in_dim(value, index, axis, keepdims=False)


def tie(*values):
    return lax.optimization_barrier(values)


def exchange(axis, chunk):
    two = shift(chunk(2), axis, 4, 2)
    one = shift(chunk(1), axis, 4, 1)
    three = shift(chunk(3), axis, 4, -1)
    return one, two, three


def column_gather(block, beside):
    (block,) = tie(block)
    behind, opposite, ahead = exchange(Y, lambda k: block)
    opposite, beside = tie(opposite, beside)
    pieces = (block, ahead, opposite, behind)
    others = []
    for piece in pieces:
        others.append(shift(piece, "core", 2, 1))
    return pieces, others, beside


def in_order(pieces, first):
    out = jnp.zeros((4, *pieces[0].shape), pieces[0].dtype)
    for i in (0, 1, 3, 2):
        out = lax.dynamic_update_slice(out, pieces[i][None], ((i - first) % 4, 0, 0))
    return out


def step(source, targets, encoder_weight, encoder_bias, decoder_weight):
    yh, core, z, x, yl = (lax.axis_index(a) for a in ("yh", "core", "z", "x", "yl"))
    half_tokens, width = source.shape
    block = half_tokens // 4
    features, columns = decoder_weight.shape[1:]
    half_columns = columns // 2
    part_columns = half_columns // 4
    scale_root = 1.0 / math.sqrt(half_tokens * 2)
    decoder = decoder_weight[0]
    target_rows = targets[0]
    column_start = yl * half_columns

    decoder_turned = jnp.concatenate(
        [
            lax.dynamic_slice(
                decoder,
                (0, column_start + part_columns * ((x + k) % 4)),
                (features, part_columns),
            )
            for k in range(4)
        ],
        axis=1,
    )

    def part(k):
        return decoder_turned[:, k * part_columns : (k + 1) * part_columns]

    source_parts = source.reshape(2, 2, block, width)
    there = pick(source_parts, 1 - core, 1)
    here = pick(source_parts, core, 1)
    there = jnp.concatenate([pick(there, 1 - yh), pick(there, yh)], axis=0)
    sent = shift(mm(there, encoder_weight).astype(bf16), "core", 2, 1).astype(f32)
    other = (mm(pick(here, 1 - yh), encoder_weight) + sent[:block]).astype(bf16)
    other = shift(other, "yh", 2, 1)
    kept = mm(pick(here, yh), encoder_weight) + (sent[block:] + encoder_bias.astype(f32))
    kept, decoder_turned = tie(kept, decoder_turned)
    active = jnp.maximum(kept + other.astype(f32), 0.0)
    squares = jnp.sum(jnp.square(decoder.astype(f32)), axis=1)
    acts_own, acts_other, squares = column_gather((active * active).astype(bf16), squares)
    acts_own, acts_other = in_order(acts_own, z), in_order(acts_other, z)

    half_width = width // 2
    source_theirs = lax.dynamic_slice_in_dim(source, (1 - yl) * half_width, half_width, 1)
    target_other = lax.dynamic_slice(
        target_rows,
        ((yh ^ (1 - yl) ^ (z // 2)) * 2 * block, (1 - yl) * half_columns + part_columns * x),
        (2 * block, part_columns),
    )
    source_theirs, target_other, acts_own = tie(source_theirs, target_other, acts_own)
    source_theirs = shift(source_theirs, "yl", 2, 1)
    pairs = [(q * 2 + i, q * 2 + 1 - i) for q in (1, 3) for i in range(2)]
    target_other = lax.ppermute(target_other, ("z", "yl"), pairs)
    acts = jnp.concatenate([acts_own, acts_other], axis=0).reshape(8 * block, features)
    usage = jnp.sum(acts.astype(f32), axis=0)

    def own_part(k):
        return mm(acts_own.reshape(4 * block, features), part(k)).astype(bf16 if k else f32)

    def other_part(k):
        return mm(acts_other[k], decoder_turned).astype(bf16 if k else f32)

    came_own = exchange("x", own_part)
    came_other = exchange("z", other_part)
    own_sum, other_sum = own_part(0), other_part(0)
    came_own, came_other, own_sum, other_sum, usage, source_theirs, target_other = tie(
        came_own, came_other, own_sum, other_sum, usage, source_theirs, target_other
    )
    own_sum = (own_sum + sum(c.astype(f32) for c in came_own)).reshape(4, block, part_columns)
    other_sum = other_sum + sum(c.astype(f32) for c in came_other)
    target_own = lax.dynamic_slice(
        target_rows,
        ((yh ^ (z // 2)) * 2 * block, column_start + part_columns * x),
        (2 * block, part_columns),
    )
    target_block = jnp.where(z % 2 == 1, target_other, target_own).reshape(2, block, part_columns)
    source_mine = lax.dynamic_slice_in_dim(source, yl * half_width, half_width, 1)
    source_mine = source_mine.reshape(2, 2, block, half_width)
    source_theirs = source_theirs.reshape(2, 2, block, half_width)
    slots = (
        pick(source_mine, yh),
        pick(source_theirs, yh ^ yl),
        pick(source_mine, 1 - yh),
        pick(source_theirs, 1 - (yh ^ yl)),
    )
    source_own = jnp.concatenate([pick(s, core) for s in slots], axis=0)
    source_other = jnp.concatenate([pick(s, 1 - core) for s in slots], axis=0)

    def other_chunk(k):
        return other_sum[:, k * part_columns : (k + 1) * part_columns]

    out_own = [own_sum[k].astype(bf16) for k in range(1, 4)]
    out_other = [other_chunk(k).astype(bf16) for k in range(1, 4)]
    out_own, out_other = tie(out_own, out_other)
    came_own = exchange("z", lambda k: out_own[k - 1])
    came_other = exchange("x", lambda k: out_other[k - 1])
    came_own, came_other = tie(came_own, came_other)
    full_own = own_sum[0] + sum(c.astype(f32) for c in came_own)
    full_other = other_chunk(0) + sum(c.astype(f32) for c in came_other)
    grad_own = ((full_own - pick(target_block, core).astype(f32)) * scale_root).astype(bf16)
    grad_other = ((full_other - pick(target_block, 1 - core).astype(f32)) * scale_root).astype(bf16)

    grad_own, grad_other = tie(grad_own, grad_other)
    squares = squares + shift(squares, "core", 2, 1)
    came_own = exchange("z", lambda k: grad_own)
    came_other = exchange("x", lambda k: grad_other)
    own_rows = jnp.zeros((4 * block, part_columns), bf16)
    other_cols = jnp.zeros((block, half_columns), bf16)
    for k in (0, 3, 1, 2):
        piece = came_own[3 - k] if k else grad_own
        own_rows = lax.dynamic_update_slice(own_rows, piece, (k * block, 0))
        piece = came_other[3 - k] if k else grad_other
        other_cols = lax.dynamic_update_slice(other_cols, piece, (0, k * part_columns))
    own_rows, other_cols, squares = tie(own_rows, other_cols, squares)
    squares = squares + shift(squares, "yh", 2, 1)
    norms = jnp.sqrt(squares + 1e-06)
    shares, axes = (own_rows, other_cols), ("x", "z")
    ahead, behind = [None] * 2, [None] * 2
    for i in range(2):
        behind[i] = shift(shares[i], axes[i], 4, 1)
    for i in range(2):
        ahead[i] = shift(shares[i], axes[i], 4, -1)
    ahead, behind = tie(ahead, behind)
    on_up = [v[: v.shape[0] // 2] for v in behind]
    on_down = [v[v.shape[0] // 2 :] for v in ahead]
    on_up, on_down = tie(on_up, on_down)
    far = []
    for i in range(2):
        up = shift(on_up[i], axes[i], 4, 1)
        down = shift(on_down[i], axes[i], 4, -1)
        far.append((up, down))
    far = [jnp.concatenate(v, axis=0) for v in far]
    own_pieces, other_pieces = [[v[i] for v in (shares, ahead, far, behind)] for i in range(2)]

    rebuilt_block = jnp.concatenate([full_own, full_other], axis=0).astype(bf16)
    rebuilt_block = rebuilt_block.reshape(2 * block, 2, part_columns // 2)
    rebuilt = jnp.zeros((4, block, part_columns // 2), bf16)
    for k in range(2):
        perm = []
        for zi in range(4):
            for xi in range(4):
                for yi in range(2):
                    s = (zi // 2) ^ k
                    to = ((2 * yi + xi // 2) * 4 + 2 * (xi % 2) + s) * 2 + (yi ^ (zi % 2))
                    perm.append(((zi * 4 + xi) * 2 + yi, to))
        piece = pick(rebuilt_block, (z // 2) ^ k, 1)
        piece = lax.ppermute(piece, ("z", "x", "yl"), perm)
        sender = z // 2
        rank = (x % 2) ^ k
        quarter = yh ^ rank ^ ((sender ^ yl) & sender)
        pieces = piece.reshape(2, 1, block, part_columns // 2)
        rebuilt = lax.dynamic_update_slice(rebuilt, pieces[0], (quarter * 2 + core, 0, 0))
        rebuilt = lax.dynamic_update_slice(rebuilt, pieces[1], (quarter * 2 + 1 - core, 0, 0))

    def feature_part(rows, weight):
        return lax.dot_general(
            rows, weight, (((1,), (1,)), ((), ())), preferred_element_type=f32
        )

    theirs = [None] * 4
    ours = jnp.zeros((4 * block, features), f32)
    for k in (0, 1, 3, 2):
        theirs[k] = feature_part(other_pieces[k], decoder_turned).astype(bf16)
        theirs[k] = shift(theirs[k], "core", 2, 1)
        ours = ours + feature_part(own_pieces[k], part(k))
    ours = ours.reshape(4, block, features) + jnp.stack(theirs).astype(f32)
    ours, acts = tie(ours, acts)
    came = exchange(Y, lambda k: pick(ours, (k - z) % 4).astype(bf16))
    feature_grad = pick(ours, -z % 4) + sum(c.astype(f32) for c in came)
    penalty = sparsity_weight * scale_root * norms
    pre_grad = ((feature_grad + penalty) * 2.0 * active).astype(bf16)

    def transposed(left, right):
        return lax.dot_general(
            left, right, (((0,), (0,)), ((), ())), preferred_element_type=f32
        )

    shrink = (sparsity_weight * scale_root * usage / norms)[:, None]
    decoder_grad = jnp.zeros((features, half_columns), f32)

    def add_part(out, k):
        cols = [v[:, k * part_columns : (k + 1) * part_columns] for v in other_pieces]
        term = transposed(acts, jnp.concatenate([own_pieces[k], *cols], axis=0))
        term = term + shrink * part(k).astype(f32)
        return lax.dynamic_update_slice(out, term, (0, ((x + k) % 4) * part_columns))

    for k in (0, 1, 3, 2):
        decoder_grad = add_part(decoder_grad, k)
    pre_grad, decoder_grad, rebuilt = tie(pre_grad, decoder_grad, rebuilt)
    pre_own, pre_other, rebuilt = column_gather(pre_grad, rebuilt)
    rebuilt = rebuilt.reshape(half_tokens, part_columns // 2)
    pre_own, pre_other = jnp.concatenate(pre_own, axis=0), jnp.concatenate(pre_other, axis=0)

    encoder_grad = transposed(source_own, pre_own) + transposed(source_other, pre_other)

    def bias_part(value):
        value = lax.dynamic_slice_in_dim(value, yl * (features // 2), features // 2, 1)
        return jnp.sum(value.astype(f32), axis=0)

    bias_grad = bias_part(pre_own) + bias_part(pre_other)
    return rebuilt[None], encoder_grad, bias_grad, decoder_grad[None]


def solution(mesh):
    fine = Mesh(mesh.devices.reshape(2, 2, 4, 4, 2), ("yh", "core", "z", "x", "yl"))
    tgt, feat = ("yh", "core"), ("z", "x")
    return jax.shard_map(
        step,
        mesh=fine,
        in_specs=(P("yl", tgt), P(tgt, "yl", None), P(tgt, feat), P(feat), P(tgt, feat, None)),
        out_specs=(
            P(tgt, "yl", feat),
            P(("yh", "core", "yl"), feat),
            P(("z", "x", "yl")),
            P(tgt, feat, "yl"),
        ),
        check_vma=False,
    )
```

```python
import math

import jax
import jax.numpy as jnp
from jax import lax
from jax.sharding import Mesh, PartitionSpec as P


sparsity_weight = 2.0

bf16 = jnp.bfloat16
f32 = jnp.float32
Y = ("yh", "yl")


def shift(value, axis, size, step):
    return lax.ppermute(value, axis, [(i, (i + step) % size) for i in range(size)])


def mm(left, right):
    return jnp.dot(left, right, preferred_element_type=f32)


def pick(value, index, axis=0):
    return lax.dynamic_index_in_dim(value, index, axis, keepdims=False)


def tie(*values):
    return lax.optimization_barrier(values)


def exchange(axis, chunk):
    two = shift(chunk(2), axis, 4, 2)
    one = shift(chunk(1), axis, 4, 1)
    three = shift(chunk(3), axis, 4, -1)
    return one, two, three


def column_gather(block, beside):
    (block,) = tie(block)
    behind, opposite, ahead = exchange(Y, lambda k: block)
    opposite, beside = tie(opposite, beside)
    pieces = (block, ahead, opposite, behind)
    others = []
    for piece in pieces:
        others.append(shift(piece, "core", 2, 1))
    return pieces, others, beside


def in_order(pieces, first):
    out = jnp.zeros((4, *pieces[0].shape), pieces[0].dtype)
    for i in (0, 1, 3, 2):
        out = lax.dynamic_update_slice(out, pieces[i][None], ((i - first) % 4, 0, 0))
    return out


def step(source, targets, encoder_weight, encoder_bias, decoder_weight):
    yh, core, z, x, yl = (lax.axis_index(a) for a in ("yh", "core", "z", "x", "yl"))
    half_tokens, width = source.shape
    block = half_tokens // 4
    features, columns = decoder_weight.shape[1:]
    half_columns = columns // 2
    part_columns = half_columns // 4
    scale_root = 1.0 / math.sqrt(half_tokens * 2)
    decoder = decoder_weight[0]
    target_rows = targets[0]
    column_start = yl * half_columns

    decoder_turned = jnp.concatenate(
        [
            lax.dynamic_slice(
                decoder,
                (0, column_start + part_columns * ((x + k) % 4)),
                (features, part_columns),
            )
            for k in range(4)
        ],
        axis=1,
    )

    def part(k):
        return decoder_turned[:, k * part_columns : (k + 1) * part_columns]

    source_parts = source.reshape(2, 2, block, width)
    there = pick(source_parts, 1 - core, 1)
    here = pick(source_parts, core, 1)
    there = jnp.concatenate([pick(there, 1 - yh), pick(there, yh)], axis=0)
    sent = shift(mm(there, encoder_weight).astype(bf16), "core", 2, 1).astype(f32)
    other = (mm(pick(here, 1 - yh), encoder_weight) + sent[:block]).astype(bf16)
    other = shift(other, "yh", 2, 1)
    kept = mm(pick(here, yh), encoder_weight) + (sent[block:] + encoder_bias.astype(f32))
    kept, decoder_turned = tie(kept, decoder_turned)
    active = jnp.maximum(kept + other.astype(f32), 0.0)
    squares = jnp.sum(jnp.square(decoder.astype(f32)), axis=1)
    acts_own, acts_other, squares = column_gather((active * active).astype(bf16), squares)
    acts_own, acts_other = in_order(acts_own, z), in_order(acts_other, z)

    half_width = width // 2
    source_theirs = lax.dynamic_slice_in_dim(source, (1 - yl) * half_width, half_width, 1)
    target_other = lax.dynamic_slice(
        target_rows,
        ((yh ^ (1 - yl) ^ (z // 2)) * 2 * block, (1 - yl) * half_columns + part_columns * x),
        (2 * block, part_columns),
    )
    source_theirs, target_other, acts_own = tie(source_theirs, target_other, acts_own)
    source_theirs = shift(source_theirs, "yl", 2, 1)
    pairs = [(q * 2 + i, q * 2 + 1 - i) for q in (1, 3) for i in range(2)]
    target_other = lax.ppermute(target_other, ("z", "yl"), pairs)
    acts = jnp.concatenate([acts_own, acts_other], axis=0).reshape(8 * block, features)
    usage = jnp.sum(acts.astype(f32), axis=0)

    def own_part(k):
        return mm(acts_own.reshape(4 * block, features), part(k)).astype(bf16 if k else f32)

    def other_part(k):
        return mm(acts_other[k], decoder_turned).astype(bf16 if k else f32)

    axes = ("x", "z")
    came_own = exchange("x", own_part)
    came_other = exchange("z", other_part)
    own_sum, other_sum = own_part(0), other_part(0)
    came_own, came_other, own_sum, other_sum, usage, source_theirs, target_other = tie(
        came_own, came_other, own_sum, other_sum, usage, source_theirs, target_other
    )
    own_sum = own_sum + sum(c.astype(f32) for c in came_own)
    other_sum = other_sum + sum(c.astype(f32) for c in came_other)
    own_sum = own_sum.reshape(4, block, part_columns)
    target_own = lax.dynamic_slice(
        target_rows,
        ((yh ^ (z // 2)) * 2 * block, column_start + part_columns * x),
        (2 * block, part_columns),
    )
    target_block = jnp.where(z % 2 == 1, target_other, target_own).reshape(2, block, part_columns)

    source_mine = lax.dynamic_slice_in_dim(source, yl * half_width, half_width, 1)
    source_mine = source_mine.reshape(2, 2, block, half_width)
    source_theirs = source_theirs.reshape(2, 2, block, half_width)
    slots = (
        pick(source_mine, yh),
        pick(source_theirs, yh ^ yl),
        pick(source_mine, 1 - yh),
        pick(source_theirs, 1 - (yh ^ yl)),
    )
    source_own = jnp.concatenate([pick(s, core) for s in slots], axis=0)
    source_other = jnp.concatenate([pick(s, 1 - core) for s in slots], axis=0)

    def other_chunk(k):
        return other_sum[:, k * part_columns : (k + 1) * part_columns]

    out_own = [own_sum[k].astype(bf16) for k in range(1, 4)]
    out_other = [other_chunk(k).astype(bf16) for k in range(1, 4)]
    out_own, out_other = tie(out_own, out_other)
    came_own = exchange("z", lambda k: out_own[k - 1])
    came_other = exchange("x", lambda k: out_other[k - 1])
    came_own, came_other = tie(came_own, came_other)
    full_own = own_sum[0] + sum(c.astype(f32) for c in came_own)
    full_other = other_chunk(0) + sum(c.astype(f32) for c in came_other)
    grad_own = ((full_own - pick(target_block, core).astype(f32)) * scale_root).astype(bf16)
    grad_other = ((full_other - pick(target_block, 1 - core).astype(f32)) * scale_root).astype(bf16)

    grad_own, grad_other = tie(grad_own, grad_other)
    squares = squares + shift(squares, "core", 2, 1)
    came_own = exchange("z", lambda k: grad_own)
    came_other = exchange("x", lambda k: grad_other)
    own_rows = jnp.zeros((4 * block, part_columns), bf16)
    other_cols = jnp.zeros((block, half_columns), bf16)
    for k in (0, 3, 1, 2):
        piece = came_own[3 - k] if k else grad_own
        own_rows = lax.dynamic_update_slice(own_rows, piece, (k * block, 0))
        piece = came_other[3 - k] if k else grad_other
        other_cols = lax.dynamic_update_slice(other_cols, piece, (0, k * part_columns))
    own_rows, other_cols, squares = tie(own_rows, other_cols, squares)
    squares = squares + shift(squares, "yh", 2, 1)
    norms = jnp.sqrt(squares + 1e-06)
    shares = (own_rows, other_cols)
    ahead, behind = [None] * 2, [None] * 2
    for i in range(2):
        behind[i] = shift(shares[i], axes[i], 4, 1)
    for i in range(2):
        ahead[i] = shift(shares[i], axes[i], 4, -1)
    ahead, behind = tie(ahead, behind)
    on_up = [v[: v.shape[0] // 2] for v in behind]
    on_down = [v[v.shape[0] // 2 :] for v in ahead]
    on_up, on_down = tie(on_up, on_down)
    far = []
    for i in range(2):
        up = shift(on_up[i], axes[i], 4, 1)
        down = shift(on_down[i], axes[i], 4, -1)
        far.append((up, down))
    far = [jnp.concatenate(v, axis=0) for v in far]
    own_pieces, other_pieces = [[v[i] for v in (shares, ahead, far, behind)] for i in range(2)]

    rebuilt_block = jnp.concatenate([full_own, full_other], axis=0).astype(bf16)
    rebuilt_block = rebuilt_block.reshape(2 * block, 2, part_columns // 2)
    rebuilt = jnp.zeros((4, block, part_columns // 2), bf16)
    for k in range(2):
        perm = []
        for zi in range(4):
            for xi in range(4):
                for yi in range(2):
                    s = (zi // 2) ^ k
                    to = ((2 * yi + xi // 2) * 4 + 2 * (xi % 2) + s) * 2 + (yi ^ (zi % 2))
                    perm.append(((zi * 4 + xi) * 2 + yi, to))
        piece = pick(rebuilt_block, (z // 2) ^ k, 1)
        piece = lax.ppermute(piece, ("z", "x", "yl"), perm)
        sender = z // 2
        rank = (x % 2) ^ k
        quarter = yh ^ rank ^ ((sender ^ yl) & sender)
        pieces = piece.reshape(2, 1, block, part_columns // 2)
        rebuilt = lax.dynamic_update_slice(rebuilt, pieces[0], (quarter * 2 + core, 0, 0))
        rebuilt = lax.dynamic_update_slice(rebuilt, pieces[1], (quarter * 2 + 1 - core, 0, 0))

    def feature_part(rows, weight):
        return lax.dot_general(
            rows, weight, (((1,), (1,)), ((), ())), preferred_element_type=f32
        )

    theirs = [None] * 4
    ours = jnp.zeros((4 * block, features), f32)
    for k in (0, 1, 3, 2):
        theirs[k] = feature_part(other_pieces[k], decoder_turned).astype(bf16)
        theirs[k] = shift(theirs[k], "core", 2, 1)
        ours = ours + feature_part(own_pieces[k], part(k))
    ours = ours.reshape(4, block, features) + jnp.stack(theirs).astype(f32)
    ours, acts = tie(ours, acts)
    came = exchange(Y, lambda k: pick(ours, (k - z) % 4).astype(bf16))
    feature_grad = pick(ours, -z % 4) + sum(c.astype(f32) for c in came)
    penalty = sparsity_weight * scale_root * norms
    pre_grad = ((feature_grad + penalty) * 2.0 * active).astype(bf16)

    def transposed(left, right):
        return lax.dot_general(
            left, right, (((0,), (0,)), ((), ())), preferred_element_type=f32
        )

    shrink = (sparsity_weight * scale_root * usage / norms)[:, None]
    decoder_grad = jnp.zeros((features, half_columns), f32)

    def add_part(out, k):
        cols = [v[:, k * part_columns : (k + 1) * part_columns] for v in other_pieces]
        term = transposed(acts, jnp.concatenate([own_pieces[k], *cols], axis=0))
        term = term + shrink * part(k).astype(f32)
        return lax.dynamic_update_slice(out, term, (0, ((x + k) % 4) * part_columns))

    for k in (0, 1, 3, 2):
        decoder_grad = add_part(decoder_grad, k)
    pre_grad, decoder_grad = tie(pre_grad, decoder_grad)
    pre_own, pre_other, rebuilt = column_gather(pre_grad, rebuilt)
    rebuilt = rebuilt.reshape(half_tokens, part_columns // 2)
    pre_own, pre_other = jnp.concatenate(pre_own, axis=0), jnp.concatenate(pre_other, axis=0)

    encoder_grad = transposed(source_own, pre_own) + transposed(source_other, pre_other)

    def bias_part(value):
        value = lax.dynamic_slice_in_dim(value, yl * (features // 2), features // 2, 1)
        return jnp.sum(value.astype(f32), axis=0)

    bias_grad = bias_part(pre_own) + bias_part(pre_other)
    return rebuilt[None], encoder_grad, bias_grad, decoder_grad[None]


def solution(mesh):
    fine = Mesh(mesh.devices.reshape(2, 2, 4, 4, 2), ("yh", "core", "z", "x", "yl"))
    tgt, feat = ("yh", "core"), ("z", "x")
    return jax.shard_map(
        step,
        mesh=fine,
        in_specs=(P("yl", tgt), P(tgt, "yl", None), P(tgt, feat), P(feat), P(tgt, feat, None)),
        out_specs=(
            P(tgt, "yl", feat),
            P(("yh", "core", "yl"), feat),
            P(("z", "x", "yl")),
            P(tgt, feat, "yl"),
        ),
        check_vma=False,
    )
```

```python
import math

import jax
import jax.numpy as jnp
from jax import lax
from jax.sharding import Mesh, PartitionSpec as P


sparsity_weight = 2.0

bf16 = jnp.bfloat16
f32 = jnp.float32
Y = ("yh", "yl")


def shift(value, axis, size, step):
    return lax.ppermute(value, axis, [(i, (i + step) % size) for i in range(size)])


def mm(left, right):
    return jnp.dot(left, right, preferred_element_type=f32)


def pick(value, index, axis=0):
    return lax.dynamic_index_in_dim(value, index, axis, keepdims=False)


def tie(*values):
    return lax.optimization_barrier(values)


def exchange(axis, chunk):
    two = shift(chunk(2), axis, 4, 2)
    one = shift(chunk(1), axis, 4, 1)
    three = shift(chunk(3), axis, 4, -1)
    return one, two, three


def column_gather(block, beside):
    (block,) = tie(block)
    behind, opposite, ahead = exchange(Y, lambda k: block)
    opposite, beside = tie(opposite, beside)
    pieces = (block, ahead, opposite, behind)
    others = []
    for piece in pieces:
        others.append(shift(piece, "core", 2, 1))
    return pieces, others, beside


def in_order(pieces, first):
    out = jnp.zeros((4, *pieces[0].shape), pieces[0].dtype)
    for i in (0, 1, 3, 2):
        out = lax.dynamic_update_slice(out, pieces[i][None], ((i - first) % 4, 0, 0))
    return out


def step(source, targets, encoder_weight, encoder_bias, decoder_weight):
    yh, core, z, x, yl = (lax.axis_index(a) for a in ("yh", "core", "z", "x", "yl"))
    half_tokens, width = source.shape
    block = half_tokens // 4
    features, columns = decoder_weight.shape[1:]
    half_columns = columns // 2
    part_columns = half_columns // 4
    scale_root = 1.0 / math.sqrt(half_tokens * 2)
    decoder = decoder_weight[0]
    target_rows = targets[0]
    column_start = yl * half_columns

    decoder_turned = jnp.concatenate(
        [
            lax.dynamic_slice(
                decoder,
                (0, column_start + part_columns * ((x + k) % 4)),
                (features, part_columns),
            )
            for k in range(4)
        ],
        axis=1,
    )

    def part(k):
        return decoder_turned[:, k * part_columns : (k + 1) * part_columns]

    source_parts = source.reshape(2, 2, block, width)
    there = pick(source_parts, 1 - core, 1)
    here = pick(source_parts, core, 1)
    there = jnp.concatenate([pick(there, 1 - yh), pick(there, yh)], axis=0)
    sent = shift(mm(there, encoder_weight).astype(bf16), "core", 2, 1).astype(f32)
    other = (mm(pick(here, 1 - yh), encoder_weight) + sent[:block]).astype(bf16)
    other = shift(other, "yh", 2, 1)
    kept = mm(pick(here, yh), encoder_weight) + (sent[block:] + encoder_bias.astype(f32))
    kept, decoder_turned = tie(kept, decoder_turned)
    active = jnp.maximum(kept + other.astype(f32), 0.0)
    squares = jnp.sum(jnp.square(decoder.astype(f32)), axis=1)
    acts_own, acts_other, squares = column_gather((active * active).astype(bf16), squares)
    acts_own, acts_other = in_order(acts_own, z), in_order(acts_other, z)

    half_width = width // 2
    source_theirs = lax.dynamic_slice_in_dim(source, (1 - yl) * half_width, half_width, 1)
    target_other = lax.dynamic_slice(
        target_rows,
        ((yh ^ (1 - yl) ^ (z // 2)) * 2 * block, (1 - yl) * half_columns + part_columns * x),
        (2 * block, part_columns),
    )
    source_theirs, target_other, acts_own = tie(source_theirs, target_other, acts_own)
    source_theirs = shift(source_theirs, "yl", 2, 1)
    pairs = [(q * 2 + i, q * 2 + 1 - i) for q in (1, 3) for i in range(2)]
    target_other = lax.ppermute(target_other, ("z", "yl"), pairs)
    acts = jnp.concatenate([acts_own, acts_other], axis=0).reshape(8 * block, features)
    usage = jnp.sum(acts.astype(f32), axis=0)

    def own_part(k):
        return mm(acts_own.reshape(4 * block, features), part(k)).astype(bf16 if k else f32)

    def other_part(k):
        return mm(acts_other[k], decoder_turned).astype(bf16 if k else f32)

    axes = ("x", "z")
    came_own = exchange("x", own_part)
    came_other = exchange("z", other_part)
    own_sum, other_sum = own_part(0), other_part(0)
    squares = squares + shift(squares, "core", 2, 1)
    squares = squares + shift(squares, "yh", 2, 1)
    came_own, came_other, own_sum, other_sum, usage, squares, source_theirs, target_other = tie(
        came_own, came_other, own_sum, other_sum, usage, squares, source_theirs, target_other
    )
    norms = jnp.sqrt(squares + 1e-06)
    own_sum = own_sum + sum(c.astype(f32) for c in came_own)
    other_sum = other_sum + sum(c.astype(f32) for c in came_other)
    own_sum = own_sum.reshape(4, block, part_columns)
    target_own = lax.dynamic_slice(
        target_rows,
        ((yh ^ (z // 2)) * 2 * block, column_start + part_columns * x),
        (2 * block, part_columns),
    )
    target_block = jnp.where(z % 2 == 1, target_other, target_own).reshape(2, block, part_columns)

    source_mine = lax.dynamic_slice_in_dim(source, yl * half_width, half_width, 1)
    source_mine = source_mine.reshape(2, 2, block, half_width)
    source_theirs = source_theirs.reshape(2, 2, block, half_width)
    slots = (
        pick(source_mine, yh),
        pick(source_theirs, yh ^ yl),
        pick(source_mine, 1 - yh),
        pick(source_theirs, 1 - (yh ^ yl)),
    )
    source_own = jnp.concatenate([pick(s, core) for s in slots], axis=0)
    source_other = jnp.concatenate([pick(s, 1 - core) for s in slots], axis=0)

    def other_chunk(k):
        return other_sum[:, k * part_columns : (k + 1) * part_columns]

    out_own = [own_sum[k].astype(bf16) for k in range(1, 4)]
    out_other = [other_chunk(k).astype(bf16) for k in range(1, 4)]
    out_own, out_other = tie(out_own, out_other)
    came_own = exchange("z", lambda k: out_own[k - 1])
    came_other = exchange("x", lambda k: out_other[k - 1])
    came_own, came_other = tie(came_own, came_other)
    full_own = own_sum[0] + sum(c.astype(f32) for c in came_own)
    full_other = other_chunk(0) + sum(c.astype(f32) for c in came_other)
    grad_own = ((full_own - pick(target_block, core).astype(f32)) * scale_root).astype(bf16)
    grad_other = ((full_other - pick(target_block, 1 - core).astype(f32)) * scale_root).astype(bf16)

    grad_own, grad_other = tie(grad_own, grad_other)
    came_own = exchange("z", lambda k: grad_own)
    came_other = exchange("x", lambda k: grad_other)
    own_rows = jnp.zeros((4 * block, part_columns), bf16)
    other_cols = jnp.zeros((block, half_columns), bf16)
    for k in (0, 3, 1, 2):
        piece = came_own[3 - k] if k else grad_own
        own_rows = lax.dynamic_update_slice(own_rows, piece, (k * block, 0))
        piece = came_other[3 - k] if k else grad_other
        other_cols = lax.dynamic_update_slice(other_cols, piece, (0, k * part_columns))
    own_rows, other_cols = tie(own_rows, other_cols)
    shares = (own_rows, other_cols)
    ahead, behind = [None] * 2, [None] * 2
    for i in range(2):
        behind[i] = shift(shares[i], axes[i], 4, 1)
    for i in range(2):
        ahead[i] = shift(shares[i], axes[i], 4, -1)
    ahead, behind = tie(ahead, behind)
    on_up = [v[: v.shape[0] // 2] for v in behind]
    on_down = [v[v.shape[0] // 2 :] for v in ahead]
    on_up, on_down = tie(on_up, on_down)
    far = []
    for i in range(2):
        up = shift(on_up[i], axes[i], 4, 1)
        down = shift(on_down[i], axes[i], 4, -1)
        far.append((up, down))
    far = [jnp.concatenate(v, axis=0) for v in far]
    own_pieces, other_pieces = [[v[i] for v in (shares, ahead, far, behind)] for i in range(2)]

    rebuilt_block = jnp.concatenate([full_own, full_other], axis=0).astype(bf16)
    rebuilt_block = rebuilt_block.reshape(2 * block, 2, part_columns // 2)
    pieces = []
    for k in range(2):
        perm = []
        for zi in range(4):
            for xi in range(4):
                for yi in range(2):
                    s = (zi // 2) ^ k
                    to = ((2 * yi + xi // 2) * 4 + 2 * (xi % 2) + s) * 2 + (yi ^ (zi % 2))
                    perm.append(((zi * 4 + xi) * 2 + yi, to))
        piece = pick(rebuilt_block, (z // 2) ^ k, 1)
        piece = lax.ppermute(piece, ("z", "x", "yl"), perm)
        pieces.append(piece.reshape(2, block, part_columns // 2))
    sender = z // 2
    first = (yh ^ (x % 2) ^ ((sender ^ yl) & sender)) == 0
    quarters = [
        jnp.where(first, pieces[0], pieces[1]),
        jnp.where(first, pieces[1], pieces[0]),
    ]
    rebuilt = jnp.concatenate(
        [jnp.where(core == i, q[0], q[1]) for q in quarters for i in range(2)], axis=0
    )

    def feature_part(rows, weight):
        return lax.dot_general(
            rows, weight, (((1,), (1,)), ((), ())), preferred_element_type=f32
        )

    theirs = [None] * 4
    ours = jnp.zeros((4 * block, features), f32)
    for k in (0, 1, 3, 2):
        theirs[k] = feature_part(other_pieces[k], decoder_turned).astype(bf16)
        theirs[k] = shift(theirs[k], "core", 2, 1)
        ours = ours + feature_part(own_pieces[k], part(k))
    ours = ours.reshape(4, block, features) + jnp.stack(theirs).astype(f32)
    ours, acts = tie(ours, acts)
    came = exchange(Y, lambda k: pick(ours, (k - z) % 4).astype(bf16))
    feature_grad = pick(ours, -z % 4) + sum(c.astype(f32) for c in came)
    penalty = sparsity_weight * scale_root * norms
    pre_grad = ((feature_grad + penalty) * 2.0 * active).astype(bf16)

    def transposed(left, right):
        return lax.dot_general(
            left, right, (((0,), (0,)), ((), ())), preferred_element_type=f32
        )

    shrink = (sparsity_weight * scale_root * usage / norms)[:, None]
    decoder_grad = jnp.zeros((features, half_columns), f32)

    def add_columns(out, k):
        cols = [v[:, k * part_columns : (k + 1) * part_columns] for v in other_pieces]
        term = transposed(acts, jnp.concatenate([own_pieces[k], *cols], axis=0))
        term = term + shrink * part(k).astype(f32)
        return lax.dynamic_update_slice(out, term, (0, ((x + k) % 4) * part_columns))

    for k in (0, 1, 3, 2):
        decoder_grad = add_columns(decoder_grad, k)
    pre_own, pre_other, _ = column_gather(pre_grad, norms)
    pre_own, pre_other = jnp.concatenate(pre_own, axis=0), jnp.concatenate(pre_other, axis=0)

    encoder_own = transposed(source_own, pre_own)
    encoder_grad = encoder_own + transposed(source_other, pre_other)

    def bias_part(value):
        value = lax.dynamic_slice_in_dim(value, yl * (features // 2), features // 2, 1)
        return jnp.sum(value.astype(f32), axis=0)

    bias_grad = bias_part(pre_own) + bias_part(pre_other)
    return rebuilt[None], encoder_grad, bias_grad, decoder_grad[None]


def solution(mesh):
    fine = Mesh(mesh.devices.reshape(2, 2, 4, 4, 2), ("yh", "core", "z", "x", "yl"))
    tgt, feat = ("yh", "core"), ("z", "x")
    return jax.shard_map(
        step,
        mesh=fine,
        in_specs=(P("yl", tgt), P(tgt, "yl", None), P(tgt, feat), P(feat), P(tgt, feat, None)),
        out_specs=(
            P(tgt, "yl", feat),
            P(("yh", "core", "yl"), feat),
            P(("z", "x", "yl")),
            P(tgt, feat, "yl"),
        ),
        check_vma=False,
    )
```
